32 devices in a mesh: batch: 4 (over y, core), proto: 8 (over z, x).
Axes of the slice: x: 2, y: 2, z: 4, core: 2. Of those that a mesh axis runs over, the one named last changes fastest.
Arguments:
- features: bfloat16 [4096, 256], P(('batch', 'proto')), may hold values from -8 to 8
- head_weight: bfloat16 [256, 65536], P('batch', 'proto'), may hold values from -0.375 to 0.375
- student_scores: bfloat16 [2, 4096, 65536], P(None, 'batch', 'proto'), may hold values from -1 to 1
Outputs:
- targets: bfloat16 [4096, 65536], P('batch', 'proto')
- row_loss: float32 [2, 4096], P(None, 'batch')
The draws below stay inside these ranges and needn't reach their ends.
All inputs are finite; a program needn't handle non-finite values.
Results may differ from the reference program's by a relative error of at most 0.0013.
Values may be sent and summed in bfloat16 or wider, within the bound.
No kernel may reach another device: no remote copies, remote signals or barrier semaphores. Data moves between devices by JAX's collectives and lax.ppermute only.
A program may use at most 192 MiB of HBM per device.

```python
import jax
import jax.numpy as jnp
from jax import lax

BOTTLENECK = 256
PROTOS = 65536
VIEWS = 2
ITERS = 3
ROWS = 4096


def centre_table(key):
    count = max(PROTOS // 1024, 4)
    centres = jax.random.normal(jax.random.fold_in(key, 101), (count, BOTTLENECK), jnp.float32)
    return (count, centres)


def draw_features(key, part):
    count, centres = centre_table(key)
    first = jax.random.randint(jax.random.fold_in(key, 21), (ROWS,), 0, count)
    second = jax.random.randint(jax.random.fold_in(key, 22), (ROWS,), 0, count)
    label = jnp.minimum(first, second).astype(jnp.int32)
    picked = centres[label]
    strength = jax.random.uniform(jax.random.fold_in(key, 23), (ROWS, 1), jnp.float32, 0.4, 1.0)
    noise = jax.random.normal(jax.random.fold_in(key, 24), (ROWS, BOTTLENECK), jnp.float32)
    values = strength * picked + noise
    return jnp.clip(values, -8.0, 8.0).astype(jnp.bfloat16)


def draw_head_weight(key, part):
    count, centres = centre_table(key)
    block = max(PROTOS // 512, 8)
    blocks = PROTOS // block
    block_label = jax.random.randint(jax.random.fold_in(key, 31), (blocks,), 0, 2 * count)
    label = jnp.repeat(block_label, block).astype(jnp.int32)
    padded = jnp.concatenate([centres, jnp.zeros((count, BOTTLENECK), jnp.float32)], axis=0)
    picked = padded[label]
    strength = jax.random.uniform(jax.random.fold_in(key, 32), (PROTOS, 1), jnp.float32, 0.5, 0.9)
    noise = jax.random.normal(jax.random.fold_in(key, 33), (PROTOS, BOTTLENECK), jnp.float32)
    values = (strength * picked + noise) * 0.05
    return jnp.clip(jnp.transpose(values), -0.375, 0.375).astype(jnp.bfloat16)


def steps_of(stream_key, extent, cuts, low, high):
    def one(axis_at, blocks):
        steps = jax.random.uniform(jax.random.fold_in(jax.random.fold_in(stream_key, 6), axis_at), (blocks,), jnp.float32, low / len(cuts), high / len(cuts))
        return jnp.repeat(jnp.exp(steps), extent[axis_at] // blocks).reshape((-1,) + (1,) * (len(extent) - axis_at - 1))

    loudness = one(*cuts[0])
    for cut in cuts[1:]:
        loudness = loudness * one(*cut)
    return loudness


def setup_inputs(seed: int = 0) -> dict:
    key_of = jax.random.split(jax.random.key(seed), 4)
    features = draw_features(jax.random.fold_in(key_of[3], 71), 0)
    head_weight = draw_head_weight(jax.random.fold_in(key_of[3], 71), 0)
    student_scores = jnp.clip(jax.random.uniform(key_of[2], (VIEWS, ROWS, PROTOS), jnp.float32, -1.0, 1.0) * steps_of(key_of[2], (VIEWS, ROWS, PROTOS), ((1, 4), (2, 8)), -0.4, 0.0), -1.0, 1.0).astype(jnp.bfloat16)
    return {"features": features, "head_weight": head_weight, "student_scores": student_scores}


TEACHER_TEMP = 0.07
STUDENT_TEMP = 0.1

def reference(features, head_weight, student_scores):
    feat_wide = features.astype(jnp.float32)
    fnorm = jnp.sqrt(lax.optimization_barrier(jnp.sum(feat_wide * feat_wide, axis=1)) + 1e-06)
    weight_wide = head_weight.astype(jnp.float32)
    wnorm = jnp.sqrt(lax.optimization_barrier(jnp.sum(weight_wide * weight_wide, axis=0)) + 1e-06)
    raw = jnp.dot(features, head_weight, preferred_element_type=jnp.float32)
    balance = jnp.exp(raw / (fnorm[:, None] * wnorm[None, :]) / TEACHER_TEMP)
    for step in range(ITERS):
        balance = balance / lax.optimization_barrier(jnp.sum(balance, axis=0, keepdims=True))
        balance = balance / lax.optimization_barrier(jnp.sum(balance, axis=1, keepdims=True))

    def one_view(view):
        logits = view.astype(jnp.float32) / STUDENT_TEMP
        lse = jnp.log(lax.optimization_barrier(jnp.sum(jnp.exp(logits), axis=1)))
        return lse - lax.optimization_barrier(jnp.sum(balance * logits, axis=1))
    row_loss = lax.map(one_view, student_scores)
    targets = (balance * PROTOS).astype(jnp.bfloat16)
    return (targets, row_loss)
```

```python
import jax
import jax.numpy as jnp
from jax import lax
from jax.experimental import pallas as pl
from jax.experimental.pallas import tpu as pltpu
from jax.sharding import PartitionSpec as P

PROTOS = 65536
TEACHER_TEMP = 0.07
STUDENT_TEMP = 0.1
LOG2E = 1.4426950408889634
LANES = 128
VMEM = pltpu.MemorySpace.VMEM
HI = lax.Precision.HIGHEST


def params(mib, grid=0):
    return pltpu.CompilerParams(
        vmem_limit_bytes=mib << 20,
        dimension_semantics=("arbitrary",) * grid if grid else None,
    )


def whole():
    return pl.BlockSpec(memory_space=VMEM)


def lane_sums(acc):
    ones = jnp.ones((8, LANES), jnp.float32)
    out = lax.dot_general(ones, acc, (((1,), (1,)), ((), ())), precision=HI,
                          preferred_element_type=jnp.float32)
    return out[0:1]


def to_rows(row):
    return jnp.transpose(jnp.broadcast_to(row, (LANES, LANES)))


def student_kernel(scores, out, acc_ref):
    i = pl.program_id(0)
    views, rows, cols = scores.shape
    sub = 16
    scale = jnp.float32(LOG2E / STUDENT_TEMP)
    for v in range(views):
        def body(r, _):
            at = pl.multiple_of(r * sub, sub)
            acc = [jnp.zeros((sub, LANES), jnp.float32) for _ in range(2)]
            for t in range(cols // LANES):
                s = scores[v, pl.ds(at, sub), t * LANES:(t + 1) * LANES].astype(jnp.float32)
                acc[t % 2] = acc[t % 2] + jnp.exp2(s * scale)
            acc_ref[pl.ds(at, sub), :] = acc[0] + acc[1]
            return 0

        lax.fori_loop(0, rows // sub, body, 0)
        out[v, pl.ds(i, 1), :] = lane_sums(acc_ref[...])


def student_sums(scores):
    views, rows, cols = scores.shape
    n = rows // LANES
    return pl.pallas_call(
        student_kernel,
        grid=(n,),
        in_specs=[pl.BlockSpec((views, LANES, cols), lambda i: (0, i, 0))],
        out_specs=pl.BlockSpec((views, n, LANES), lambda i: (0, 0, 0)),
        out_shape=jax.ShapeDtypeStruct((views, n, LANES), jnp.float32),
        scratch_shapes=[pltpu.VMEM((LANES, LANES), jnp.float32)],
        compiler_params=params(10, 1),
        cost_estimate=pl.CostEstimate(flops=views * rows * cols * 4, transcendentals=views * rows * cols,
                                      bytes_accessed=views * rows * cols * 2),
        name="student_exp",
    )(scores)


def kernel_block(nblocks, step, refs):
    feats = refs[0]
    weights = refs[1:1 + nblocks]
    kmat, csum, fscale = refs[1 + nblocks:]
    rows = feats.shape[0]
    cols = csum.shape[1]
    sub = 128

    def norms(r, _):
        at = pl.multiple_of(r * sub, sub)
        f = feats[pl.ds(at, sub), :].astype(jnp.float32)
        total = jnp.sum(f * f, axis=1, keepdims=True)
        fscale[pl.ds(at, sub), :] = jnp.broadcast_to(
            (LOG2E / TEACHER_TEMP) / jnp.sqrt(total + 1e-06), (sub, LANES))
        return 0

    lax.fori_loop(0, rows // sub, norms, 0)

    def block(c, _):
        at = pl.multiple_of(c * step, step)
        w = jnp.concatenate([ref[:, pl.ds(at, step)] for ref in weights], axis=0)
        wide = w.astype(jnp.float32)
        wscale = 1.0 / jnp.sqrt(jnp.sum(wide * wide, axis=0, keepdims=True) + 1e-06)

        def row_block(r, acc):
            rt = pl.multiple_of(r * sub, sub)
            raw = jnp.dot(feats[pl.ds(rt, sub), :], w, preferred_element_type=jnp.float32)
            fs = fscale[pl.ds(rt, sub), :]
            k = jnp.exp2(raw * jnp.concatenate([fs] * (step // LANES), axis=1) * wscale)
            kmat[pl.ds(rt, sub), pl.ds(at, step)] = k
            return acc + jnp.sum(k.reshape(sub // 8, 8, step), axis=0)

        acc = lax.fori_loop(0, rows // sub, row_block, jnp.zeros((8, step), jnp.float32))
        csum[:, pl.ds(at, step)] = jnp.sum(acc, axis=0, keepdims=True)
        return 0

    lax.fori_loop(0, cols // step, block, 0)


def make_kernel(feats, weights):
    rows = feats.shape[0]
    cols = weights[0].shape[1]
    step = 256
    return pl.pallas_call(
        lambda *refs: kernel_block(len(weights), step, refs),
        in_specs=[whole()] * (1 + len(weights)),
        out_specs=(whole(), whole()),
        out_shape=(pltpu.VMEM((rows, cols), jnp.float32), jax.ShapeDtypeStruct((1, cols), jnp.float32)),
        scratch_shapes=[pltpu.VMEM((rows, LANES), jnp.float32)],
        compiler_params=params(4),
        cost_estimate=pl.CostEstimate(flops=2 * rows * cols * feats.shape[1], transcendentals=rows * cols,
                                      bytes_accessed=cols * 512),
        name="teacher_kernel",
    )(feats, *weights)


def row_pass_kernel(n, refs):
    csums, kmats, out, inv, acc_ref = refs[:n], refs[n:2 * n], refs[2 * n], refs[2 * n + 1], refs[2 * n + 2]
    rows, cols = kmats[0].shape
    sub = 32
    for q in range(n):
        inv[:, q * cols:(q + 1) * cols] = 1.0 / csums[q][...]

    def body(r, _):
        at = pl.multiple_of(r * sub, sub)
        acc = [jnp.zeros((sub, LANES), jnp.float32) for _ in range(2)]
        for q in range(n):
            for t in range(cols // LANES):
                v = inv[:, q * cols + t * LANES:q * cols + (t + 1) * LANES]
                acc[t % 2] = acc[t % 2] + kmats[q][pl.ds(at, sub), t * LANES:(t + 1) * LANES] * v
        acc_ref[pl.ds(at, sub), :] = acc[0] + acc[1]
        return 0

    lax.fori_loop(0, rows // sub, body, 0)
    peers = out.shape[0]
    for i in range(rows // LANES):
        total = lane_sums(acc_ref[i * LANES:(i + 1) * LANES, :])
        for p in range(peers):
            out[p, i:i + 1, :] = total


def row_pass(csums, kmats, peers):
    rows, cols = kmats[0].shape
    n = len(kmats)
    return pl.pallas_call(
        lambda *refs: row_pass_kernel(n, refs),
        in_specs=[whole()] * (2 * n),
        out_specs=whole(),
        out_shape=jax.ShapeDtypeStruct((peers, rows // LANES, LANES), jnp.float32),
        scratch_shapes=[pltpu.VMEM((1, n * cols), jnp.float32), pltpu.VMEM((rows, LANES), jnp.float32)],
        compiler_params=params(2),
        name="row_pass",
    )(*csums, *kmats)


def col_pass_kernel(n, refs):
    rsums, kmats, outs, ub = refs[0], refs[1:1 + n], refs[1 + n:1 + 2 * n], refs[1 + 2 * n]
    rows, cols = kmats[0].shape
    u = 1.0 / jnp.sum(rsums[...], axis=0)
    for i in range(rows // LANES):
        ub[i * LANES:(i + 1) * LANES, :] = to_rows(u[i:i + 1, :])
    tiles = 8
    step = tiles * LANES
    unroll = 8
    for q in range(n):
        for c in range(cols // step):
            def body(r, acc):
                acc = list(acc)
                for j in range(unroll):
                    at = pl.multiple_of(r * 8 * unroll + j * 8, 8)
                    scale = ub[pl.ds(at, 8), :]
                    for t in range(tiles):
                        lo = c * step + t * LANES
                        acc[t] = acc[t] + kmats[q][pl.ds(at, 8), lo:lo + LANES] * scale
                return tuple(acc)

            acc = lax.fori_loop(0, rows // (8 * unroll), body,
                                tuple(jnp.zeros((8, LANES), jnp.float32) for _ in range(tiles)))
            for t in range(tiles):
                lo = c * step + t * LANES
                outs[q][:, lo:lo + LANES] = jnp.sum(acc[t], axis=0, keepdims=True)


def col_pass(rsums, kmats):
    rows, cols = kmats[0].shape
    n = len(kmats)
    return pl.pallas_call(
        lambda *refs: col_pass_kernel(n, refs),
        in_specs=[whole()] * (1 + n),
        out_specs=(whole(),) * n,
        out_shape=(jax.ShapeDtypeStruct((1, cols), jnp.float32),) * n,
        scratch_shapes=[pltpu.VMEM((rows, LANES), jnp.float32)],
        compiler_params=params(2),
        name="col_pass",
    )(rsums, *kmats)


def loss_pass_kernel(n, refs):
    scores, esums = refs[0], refs[1]
    csums, kmats = refs[2:2 + n], refs[2 + n:2 + 2 * n]
    out, inv, acc_ref = refs[2 + 2 * n:]
    i = pl.program_id(0)
    views = scores.shape[0]
    cols = kmats[0].shape[1]
    sub = 16

    @pl.when(i == 0)
    def _():
        for q in range(n):
            inv[:, q * cols:(q + 1) * cols] = 1.0 / csums[q][...]
        for v in range(views):
            for p in range(out.shape[0]):
                out[p, 1 + views + v] = esums[v]

    def body(r, _):
        rt = pl.multiple_of(r * sub, sub)
        at = pl.multiple_of(i * LANES + r * sub, sub)
        acc = [jnp.zeros((sub, LANES), jnp.float32) for _ in range(1 + views)]
        for q in range(n):
            for t in range(cols // LANES):
                lo = q * cols + t * LANES
                k = kmats[q][pl.ds(at, sub), t * LANES:(t + 1) * LANES] * inv[:, lo:lo + LANES]
                acc[0] = acc[0] + k
                for v in range(views):
                    s = scores[v, pl.ds(rt, sub), lo:lo + LANES].astype(jnp.float32)
                    acc[1 + v] = acc[1 + v] + k * s
        for m in range(1 + views):
            acc_ref[m, pl.ds(rt, sub), :] = acc[m]
        return 0

    lax.fori_loop(0, LANES // sub, body, 0)
    for m in range(1 + views):
        total = lane_sums(acc_ref[m])
        for p in range(out.shape[0]):
            out[p, m, pl.ds(i, 1), :] = total


def loss_pass(scores, esums, csums, kmats, peers):
    views, rows, cols = scores.shape
    n = len(kmats)
    nb = rows // LANES
    return pl.pallas_call(
        lambda *refs: loss_pass_kernel(n, refs),
        grid=(nb,),
        in_specs=[pl.BlockSpec((views, LANES, cols), lambda i: (0, i, 0))] + [whole()] * (1 + 2 * n),
        out_specs=pl.BlockSpec((peers, 1 + 2 * views, nb, LANES), lambda i: (0, 0, 0, 0)),
        out_shape=jax.ShapeDtypeStruct((peers, 1 + 2 * views, nb, LANES), jnp.float32),
        scratch_shapes=[pltpu.VMEM((1, cols), jnp.float32), pltpu.VMEM((1 + views, LANES, LANES), jnp.float32)],
        compiler_params=params(10, 1),
        name="loss_pass",
    )(scores, esums, *csums, *kmats)


def target_kernel(n, refs):
    stats = refs[0]
    csums, kmats = refs[1:1 + n], refs[1 + n:1 + 2 * n]
    out, loss, inv, ub = refs[1 + 2 * n:]
    i = pl.program_id(0)
    cols = kmats[0].shape[1]
    nb = stats.shape[2]
    views = loss.shape[0]
    sub = 16

    @pl.when(i == 0)
    def _():
        for q in range(n):
            inv[:, q * cols:(q + 1) * cols] = 1.0 / csums[q][...]
        total = jnp.sum(stats[...], axis=0)
        u = PROTOS / total[0]
        for b in range(nb):
            ub[b * LANES:(b + 1) * LANES, :] = to_rows(u[b:b + 1, :])
        for v in range(views):
            row = jnp.log(total[1 + views + v]) - total[1 + v] / STUDENT_TEMP / total[0]
            for b in range(nb):
                loss[v:v + 1, b * LANES:(b + 1) * LANES] = row[b:b + 1, :]

    def body(r, _):
        rt = pl.multiple_of(r * sub, sub)
        at = pl.multiple_of(i * LANES + r * sub, sub)
        scale = ub[pl.ds(at, sub), :]
        for q in range(n):
            for t in range(cols // LANES):
                lo = q * cols + t * LANES
                k = kmats[q][pl.ds(at, sub), t * LANES:(t + 1) * LANES] * inv[:, lo:lo + LANES]
                out[pl.ds(rt, sub), lo:lo + LANES] = (k * scale).astype(jnp.bfloat16)
        return 0

    lax.fori_loop(0, LANES // sub, body, 0)


def target_pass(stats, csums, kmats, views):
    rows, cols = kmats[0].shape
    n = len(kmats)
    nb = rows // LANES
    return pl.pallas_call(
        lambda *refs: target_kernel(n, refs),
        grid=(nb,),
        in_specs=[whole()] * (1 + 2 * n),
        out_specs=(pl.BlockSpec((LANES, n * cols), lambda i: (i, 0)),
                   pl.BlockSpec((views, rows), lambda i: (0, 0))),
        out_shape=(jax.ShapeDtypeStruct((rows, n * cols), jnp.bfloat16),
                   jax.ShapeDtypeStruct((views, rows), jnp.float32)),
        scratch_shapes=[pltpu.VMEM((1, n * cols), jnp.float32), pltpu.VMEM((rows, LANES), jnp.float32)],
        compiler_params=params(6, 1),
        name="target_pass",
    )(stats, *csums, *kmats)


def xor_pairs(n, mask):
    return [(i, i ^ mask) for i in range(n)]


def program(nbatch, nproto):
    bits = nbatch.bit_length() - 1
    assert 1 << bits == nbatch
    chunks = 4

    def sum_batch(arrays):
        for b in range(bits):
            pairs = xor_pairs(nbatch, 1 << b)
            arrays = [a + lax.ppermute(a, "batch", pairs) for a in arrays]
        return arrays

    def sum_columns(arrays):
        joined = sum_batch([jnp.concatenate(arrays, axis=1)])[0]
        return jnp.split(joined, len(arrays), axis=1)

    def local(features, head_weight, student_scores):
        student_scores = pltpu.with_memory_space_constraint(student_scores, pltpu.MemorySpace.HBM)
        me = lax.axis_index("batch")
        depth, cols = head_weight.shape
        cc = cols // chunks
        masks = [0]
        parts = [[head_weight[:, q * cc:(q + 1) * cc]] for q in range(chunks)]
        for b in reversed(range(bits)):
            pairs = xor_pairs(nbatch, 1 << b)
            for q in range(chunks):
                parts[q] = parts[q] + [lax.ppermute(w, "batch", pairs) for w in parts[q]]
            masks = masks + [m ^ (1 << b) for m in masks]
        mine = jnp.concatenate(
            [lax.dynamic_slice_in_dim(features, (me ^ m) * depth, depth, 1) for m in masks], axis=1)
        copies = jnp.broadcast_to(mine[None], (nproto,) + mine.shape)
        gathered = lax.all_to_all(copies, "proto", 0, 0).reshape(-1, mine.shape[1])
        esums = student_sums(student_scores)
        gathered, esums = lax.optimization_barrier((gathered, esums))

        kmats, csums = zip(*[make_kernel(gathered, parts[q]) for q in range(chunks)])
        for step in range(2):
            csums = sum_columns(csums)
            rsums = row_pass(csums, kmats, nproto)
            rsums = lax.all_to_all(rsums, "proto", 0, 0)
            csums = col_pass(rsums, kmats)
        csums = sum_columns(csums)
        stats = loss_pass(student_scores, esums, csums, kmats, nproto)
        stats = lax.all_to_all(stats, "proto", 0, 0)
        return target_pass(stats, csums, kmats, student_scores.shape[0])

    return local


def solution(mesh):
    return jax.shard_map(
        program(mesh.shape["batch"], mesh.shape["proto"]),
        mesh=mesh,
        in_specs=(P(("batch", "proto"), None), P("batch", "proto"), P(None, "batch", "proto")),
        out_specs=(P("batch", "proto"), P(None, "batch")),
        check_vma=False,
    )
```
